32 devices in a mesh: depth: 8 (over z, x), row: 4 (over y, core).
Axes of the slice: x: 2, y: 2, z: 4, core: 2. Of those that a mesh axis runs over, the one named last changes fastest.
Arguments:
- volume: float32 [8, 225, 16, 128], P('depth', None, 'row'), may hold values from -6 to 6
- measured: float32 [225, 16, 128], P(None, 'row'), may hold values from -6 to 6
- kernel_bank: float32 [8, 8, 25], P('depth'), may hold values from -0.4375 to 0.4375
- kernel_index: int32 [8, 225], P('depth'), may hold values from 0 to 7
- taps: float32 [21], replicated, may hold values from -1.5 to 1.5
- thresholds: float32 [225], replicated, may hold values from 0.05 to 0.5
Outputs:
- new_volume: float32 [8, 225, 16, 128], P('depth', None, 'row')
The draws below stay inside these ranges and needn't reach their ends.
All inputs are finite; a program needn't handle non-finite values.
Results may differ from the reference program's by a relative error of at most 0.0003.
Values sent between devices are 32-bit elements; how exact they have to be, the bound alone decides.
A program may use at most 64 MiB of HBM per device.

```python
import math
import jax
import jax.numpy as jnp
from jax import lax

P_SIZE = 225
KS = 5
TAPS = 21
NK = 8
NT = 128
Z = 8
NS = 16


def plant(result, own_key, low, largest):
    extent = result.shape
    place = [jax.random.randint(jax.random.fold_in(own_key, axis), (), 0, extent[axis]) for axis in range(len(extent))]
    result = result.at[tuple(place)].set(low)
    longest = extent.index(max(extent))
    place[longest] = (place[longest] + 1) % extent[longest]
    return result.at[tuple(place)].set(largest)


def block_scale(key, extent, shards, least, largest):
    level, own = 1.0, jax.random.fold_in(key, 6)
    for axis_at, shards_of in shards:
        steps = jnp.exp(jax.random.uniform(jax.random.fold_in(own, axis_at), (shards_of,), jnp.float32, least / len(shards), largest / len(shards)))
        level = level * jnp.repeat(steps, extent[axis_at] // shards_of).reshape([-1 if axis == axis_at else 1 for axis in range(len(extent))])
    return level


def bell_draw(rng, dims, width, bound, shards=(), held_as=jnp.bfloat16):
    level = block_scale(rng, dims, shards, -0.22, 0.18) if shards else 1.0
    array = jax.random.normal(rng, dims, jnp.float32) * width * level
    return jnp.minimum(jnp.maximum(array, -bound), bound).astype(held_as)


def setup_inputs(seed: int = 0) -> dict:
    streams_of = jax.random.split(jax.random.key(seed), 7)
    volume = bell_draw(streams_of[0], (Z, P_SIZE, NS, NT), 1.0, 6.0, ((0, 8), (2, 4)), jnp.float32)
    measured = bell_draw(streams_of[1], (P_SIZE, NS, NT), 1.0, 6.0, ((1, 4),), jnp.float32)
    kernel_bank = bell_draw(streams_of[2], (Z, NK, KS * KS), (KS * KS * Z) ** -0.5, 0.4375, ((0, 8),), jnp.float32)
    kernel_index = plant(jax.random.randint(streams_of[3], (Z, P_SIZE), 0, NK), jax.random.fold_in(streams_of[3], 1), 0, NK - 1).astype(jnp.int32)
    taps = bell_draw(streams_of[4], (TAPS,), 0.3, 1.5, (), jnp.float32)
    thresholds = jnp.clip(jnp.exp(jax.random.uniform(streams_of[5], (P_SIZE,), jnp.float32, math.log(0.05), math.log(0.5))), 0.05, 0.5)
    return dict(volume=volume, measured=measured, kernel_bank=kernel_bank, kernel_index=kernel_index, taps=taps, thresholds=thresholds)


STEP = 4.0


def kernels(kernel_bank, kernel_index):
    onehot = (kernel_index[:, :, None] == jnp.arange(NK, dtype=jnp.int32)[None, None, :]).astype(jnp.float32)
    return jnp.einsum("zpk,zkt->zpt", onehot, kernel_bank, precision=lax.Precision.HIGHEST)


def reference(volume, measured, kernel_bank, kernel_index, taps, thresholds):
    kernel = kernels(kernel_bank, kernel_index)

    def project(total, pair):
        plane, weights = pair
        padded = jnp.pad(plane, ((0, 0), (2, 2), (2, 2)))
        for a in range(KS):
            for b in range(KS):
                total = total + weights[:, a * KS + b, None, None] * padded[:, a:a + NS, b:b + NT]
        return total, None

    projection, _ = lax.scan(project, jnp.zeros((P_SIZE, NS, NT), jnp.float32), (volume, kernel))
    residual = measured - projection
    padded_res = jnp.pad(residual, ((0, 0), (2, 2), (2, 2)))

    def adjoint(weights):
        total = jnp.zeros((P_SIZE, NS, NT), jnp.float32)
        for a in range(KS):
            for b in range(KS):
                total = total + weights[:, a * KS + b, None, None] * padded_res[:, 4 - a:4 - a + NS, 4 - b:4 - b + NT]
        return total

    back = lax.map(adjoint, kernel)
    updated = volume + STEP * back
    padded_up = jnp.pad(updated, ((10, 10), (0, 0), (0, 0), (0, 0)))
    filtered = jnp.zeros_like(updated)
    for j in range(TAPS):
        filtered = filtered + taps[j] * padded_up[j:j + Z]
    return jnp.sign(filtered) * jnp.maximum(jnp.abs(filtered) - thresholds[None, :, None, None], 0.0)
```

```python
import functools

import jax
import jax.numpy as jnp
from jax import lax
from jax.experimental import pallas as pl
from jax.experimental.pallas import tpu as pltpu
from jax.sharding import PartitionSpec as P

STEP = 4.0
SIDE = 5
MESH = pl.DeviceIdType.MESH


def kernel(
    count,
    nrows,
    per,
    vol,
    meas,
    bank,
    idx,
    taps,
    lim,
    out,
    vbuf,
    mbuf,
    bbuf,
    ibuf,
    kc,
    kb,
    gb,
    vt,
    acc,
    part,
    halo,
    rsh,
    fbuf,
    vsend,
    vrecv,
    bsend,
    brecv,
    isend,
    irecv,
    fsend,
    frecv,
    hsend,
    hrecv,
    local,
):
    phases, rows, cols = vol.shape[1:]
    groups = vbuf.shape[1] // 8
    nk = bank.shape[1]
    pad = SIDE // 2
    ext = rows + 2 * pad
    half = ext // 2
    me = lax.axis_index("depth")
    row = lax.axis_index("row")

    def first_of(d):
        return jnp.minimum(d * per, phases - per)

    first = first_of(me)

    def peer(k):
        return lax.rem(me + k, count)

    def source(k):
        return lax.rem(me + count - k, count)

    def remote(src, dst, ssem, rsem, k):
        return pltpu.make_async_remote_copy(
            src_ref=src,
            dst_ref=dst,
            send_sem=ssem,
            recv_sem=rsem,
            device_id={"depth": peer(k)},
            device_id_type=MESH,
        )

    def vol_copy(k, slot):
        return remote(
            vol.at[0, pl.ds(first_of(peer(k)), per)],
            vbuf.at[slot, pl.ds(0, per)],
            vsend.at[k],
            vrecv.at[k],
            k,
        )

    def bank_copy(k, slot):
        return remote(bank.at[0], bbuf.at[slot], bsend.at[k], brecv.at[k], k)

    def idx_copy(k, slot):
        return remote(idx, ibuf.at[slot], isend.at[k], irecv.at[k], k)

    def out_copy(k, slot):
        return remote(
            fbuf.at[peer(k), pl.ds(0, per)], out.at[slot], fsend.at[k], frecv.at[k], k
        )

    own_vol = pltpu.make_async_copy(
        vol.at[0, pl.ds(first, per)], vbuf.at[me, pl.ds(0, per)], local.at[0]
    )
    own_meas = pltpu.make_async_copy(
        meas.at[pl.ds(first, per)], mbuf.at[pl.ds(0, per)], local.at[1]
    )
    own_bank = pltpu.make_async_copy(bank.at[0], bbuf.at[me], local.at[2])
    own_idx = pltpu.make_async_copy(idx, ibuf.at[me], local.at[3])
    for copy in (own_vol, own_meas, own_bank, own_idx):
        copy.start()

    barrier = pltpu.get_barrier_semaphore()

    def greet(k, carry):
        pl.semaphore_signal(
            barrier, inc=1, device_id={"depth": peer(k)}, device_id_type=MESH
        )
        return carry

    lax.fori_loop(1, count, greet, 0)
    for other in (lax.rem(row + 1, nrows), lax.rem(row + nrows - 1, nrows)):
        pl.semaphore_signal(
            barrier, inc=1, device_id={"row": other}, device_id_type=MESH
        )
    pl.semaphore_wait(barrier, count + 1)

    def send_small(k, carry):
        bank_copy(k, me).start()
        idx_copy(k, me).start()
        return carry

    def send_vol(k, carry):
        vol_copy(k, me).start()
        return carry

    lax.fori_loop(1, count, send_small, 0)
    lax.fori_loop(1, count, send_vol, 0)

    own_bank.wait()
    own_idx.wait()

    def small_in(k, carry):
        bank_copy(k, source(k)).wait_recv()
        idx_copy(k, source(k)).wait_recv()
        return carry

    lax.fori_loop(1, count, small_in, 0)

    lane = lax.broadcasted_iota(jnp.int32, (8, phases), 1)
    sub = lax.broadcasted_iota(jnp.int32, (8, phases), 0)

    def picks(g):
        return lane == first + g * 8 + sub

    def compact(z, carry):
        for g in range(groups):
            row_of = jnp.broadcast_to(ibuf[z], (8, phases))
            which = jnp.sum(
                jnp.where(picks(g), row_of.astype(jnp.float32), 0.0), axis=1, keepdims=True
            )
            total = jnp.zeros((8, SIDE * SIDE), jnp.float32)
            for n in range(nk):
                line = jnp.broadcast_to(bbuf[z, n : n + 1, :], (8, SIDE * SIDE))
                total = jnp.where(which == float(n), line, total)
            kc[z, g * 8 : g * 8 + 8, :] = total
        return carry

    lax.fori_loop(0, count, compact, 0)

    reach = taps.shape[0] // 2

    def spread(z, carry):
        for g in range(groups):
            block = kc[z, g * 8 : g * 8 + 8, :]
            for ab in range(SIDE * SIDE):
                kb[z, ab, g * 8 : g * 8 + 8, :] = jnp.broadcast_to(
                    block[:, ab : ab + 1], (8, cols)
                )
        return carry

    lax.fori_loop(0, count, spread, 0)

    def spread_mixed(zo):
        for g in range(groups):
            block = jnp.zeros((8, SIDE * SIDE), jnp.float32)
            for z in range(max(0, zo - reach), min(count, zo + reach + 1)):
                block = block + (STEP * taps[z - zo + reach]) * kc[z, g * 8 : g * 8 + 8, :]
            for ab in range(SIDE * SIDE):
                gb[zo, ab, g * 8 : g * 8 + 8, :] = jnp.broadcast_to(
                    block[:, ab : ab + 1], (8, cols)
                )

    for zo in range(count):
        spread_mixed(zo)

    acc[...] = jnp.zeros_like(acc)

    def project(z):
        def group(g, carry):
            at = pl.ds(pl.multiple_of(g * 8, 8), 8)
            lines = [vbuf[z, at, s, :] for s in range(rows)]
            for s in range(rows):
                vt[z, s, at, :] = lines[s]
            for b in range(SIDE):
                weight = [kb[z, a * SIDE + b, at, :] for a in range(SIDE)]
                for o in range(ext):
                    total = acc[b, o, at, :]
                    for a in range(SIDE):
                        s = o - 2 * pad + a
                        if 0 <= s < rows:
                            total = total + weight[a] * lines[s]
                    acc[b, o, at, :] = total
            return carry

        lax.fori_loop(0, groups, group, 0)

    own_vol.wait()
    project(me)

    def arrive(k, carry):
        vol_copy(k, source(k)).wait_recv()
        project(source(k))
        return carry

    lax.fori_loop(1, count, arrive, 0)

    t = lax.broadcasted_iota(jnp.int32, (8, cols), 1)

    def shifted(x, by):
        if by == 0:
            return x
        inside = (t + by >= 0) & (t + by < cols)
        return jnp.where(inside, pltpu.roll(x, (-by) % cols, 1), 0.0)

    own_meas.wait()

    def finish(g, carry):
        at = pl.ds(pl.multiple_of(g * 8, 8), 8)
        for o in range(ext):
            total = acc[pad, o, at, :]
            for b in range(SIDE):
                if b != pad:
                    total = total + shifted(acc[b, o, at, :], b - pad)
            if pad <= o < pad + rows:
                part[o, at, :] = mbuf[at, o - pad, :] - total
            else:
                part[o, at, :] = -total
        return carry

    lax.fori_loop(0, groups, finish, 0)

    down = pltpu.make_async_remote_copy(
        src_ref=part.at[pl.ds(half, half)],
        dst_ref=halo.at[pl.ds(0, half)],
        send_sem=hsend.at[0],
        recv_sem=hrecv.at[0],
        device_id={"row": lax.rem(row + 1, nrows)},
        device_id_type=MESH,
    )
    up = pltpu.make_async_remote_copy(
        src_ref=part.at[pl.ds(0, half)],
        dst_ref=halo.at[pl.ds(half, half)],
        send_sem=hsend.at[1],
        recv_sem=hrecv.at[1],
        device_id={"row": lax.rem(row + nrows - 1, nrows)},
        device_id_type=MESH,
    )
    has_prev = row > 0
    has_next = row < nrows - 1

    @pl.when(has_next)
    def _():
        down.start()

    @pl.when(has_prev)
    def _():
        up.start()

    def axial(i, carry):
        g = lax.div(i, rows)
        s = lax.rem(i, rows)
        at = pl.ds(pl.multiple_of(g * 8, 8), 8)
        planes = [vt[z, s, at, :] for z in range(count)]
        for zo in range(count):
            total = None
            for z in range(max(0, zo - reach), min(count, zo + reach + 1)):
                term = taps[z - zo + reach] * planes[z]
                total = term if total is None else total + term
            vt[zo, s, at, :] = total
        return carry

    lax.fori_loop(0, groups * rows, axial, 0)

    limits = []
    for g in range(groups):
        line = jnp.broadcast_to(lim[...], (8, phases))
        limits.append(
            jnp.broadcast_to(
                jnp.sum(jnp.where(picks(g), line, 0.0), axis=1, keepdims=True), (8, cols)
            )
        )

    @pl.when(has_prev)
    def _():
        down.wait_recv()

    @pl.when(has_next)
    def _():
        up.wait_recv()

    def residual(g, carry):
        at = pl.ds(pl.multiple_of(g * 8, 8), 8)
        for o in range(ext):
            there = has_prev if o < half else has_next
            got = jnp.where(there, halo[o, at, :], 0.0)
            total = part[o, at, :] + got
            if o < pad or o >= pad + rows:
                total = jnp.where(there, total, 0.0)
            for b in range(SIDE):
                rsh[b, o, at, :] = shifted(total, pad - b)
        return carry

    lax.fori_loop(0, groups, residual, 0)

    def back(z):
        for g in range(groups):
            at = pl.ds(g * 8, 8)
            totals = [vt[z, s, at, :] for s in range(rows)]
            for b in range(SIDE):
                shift = [rsh[b, o, at, :] for o in range(ext)]
                for a in range(SIDE):
                    weight = gb[z, a * SIDE + b, at, :]
                    for s in range(rows):
                        totals[s] = totals[s] + weight * shift[s - a + 2 * pad]
            for s in range(rows):
                value = totals[s]
                size = jnp.maximum(jnp.abs(value) - limits[g], 0.0)
                fbuf[z, at, s, :] = jnp.where(value < 0.0, -size, size)

    def give(k, carry):
        back(peer(k))
        out_copy(k, me).start()
        return carry

    lax.fori_loop(1, count, give, 0)
    back(me)
    own_out = pltpu.make_async_copy(fbuf.at[me, pl.ds(0, per)], out.at[me], local.at[4])
    own_out.start()

    def drain(k, carry):
        bank_copy(k, me).wait_send()
        idx_copy(k, me).wait_send()
        vol_copy(k, me).wait_send()
        out_copy(k, me).wait_send()
        return carry

    def collect(k, carry):
        out_copy(k, source(k)).wait_recv()
        return carry

    @pl.when(has_next)
    def _():
        down.wait_send()

    @pl.when(has_prev)
    def _():
        up.wait_send()

    own_out.wait()
    lax.fori_loop(1, count, drain, 0)
    lax.fori_loop(1, count, collect, 0)


def shards(count, nrows, volume, measured, kernel_bank, kernel_index, taps, thresholds):
    planes, phases, rows, cols = volume.shape
    nk, size = kernel_bank.shape[1:]
    per = -(-phases // count)
    wide = -(-per // 8) * 8
    ext = rows + SIDE - 1
    f32 = jnp.float32
    dma = pltpu.SemaphoreType.DMA
    vmem = pl.BlockSpec(memory_space=pltpu.VMEM)
    smem = pl.BlockSpec(memory_space=pltpu.SMEM)
    hbm = pl.BlockSpec(memory_space=pl.ANY)
    got = pl.pallas_call(
        functools.partial(kernel, count, nrows, per),
        out_shape=jax.ShapeDtypeStruct((count, per, rows, cols), f32),
        in_specs=[hbm, hbm, vmem, vmem, smem, vmem],
        out_specs=hbm,
        scratch_shapes=[
            pltpu.VMEM((count, wide, rows, cols), f32),
            pltpu.VMEM((wide, rows, cols), f32),
            pltpu.VMEM((count, nk, size), f32),
            pltpu.VMEM((count, 1, phases), jnp.int32),
            pltpu.VMEM((count, wide, size), f32),
            pltpu.VMEM((count, size, wide, cols), f32),
            pltpu.VMEM((count, size, wide, cols), f32),
            pltpu.VMEM((count, rows, wide, cols), f32),
            pltpu.VMEM((SIDE, ext, wide, cols), f32),
            pltpu.VMEM((ext, wide, cols), f32),
            pltpu.VMEM((ext, wide, cols), f32),
            pltpu.VMEM((SIDE, ext, wide, cols), f32),
            pltpu.VMEM((count, wide, rows, cols), f32),
        ]
        + [dma((count,)) for _ in range(8)]
        + [dma((2,)), dma((2,)), dma((5,))],
        compiler_params=pltpu.CompilerParams(collective_id=0, has_side_effects=True),
    )(volume, measured, kernel_bank, kernel_index, taps, thresholds[None, :])
    full = phases // per
    rest = phases - full * per
    lines = got.reshape(count * per, rows, cols)
    if rest:
        stop = (full + 1) * per
        lines = jnp.concatenate([lines[: full * per], lines[stop - rest : stop]], 0)
    return lines[None, :phases]


def solution(mesh):
    placed = (
        P("depth", None, "row", None),
        P(None, "row", None),
        P("depth", None, None),
        P("depth", None),
        P(),
        P(),
    )
    body = functools.partial(shards, mesh.shape["depth"], mesh.shape["row"])
    return jax.shard_map(
        body, mesh=mesh, in_specs=placed, out_specs=P("depth", None, "row", None), check_vma=False
    )
```

```python
import functools

import jax
import jax.numpy as jnp
from jax import lax
from jax.experimental import pallas as pl
from jax.experimental.pallas import tpu as pltpu
from jax.sharding import PartitionSpec as P

STEP = 4.0
SIDE = 5
CHUNKS = 2
MESH = pl.DeviceIdType.MESH


def kernel(
    count,
    nrows,
    per,
    chunks,
    vol,
    meas,
    bank,
    idx,
    taps,
    lim,
    out,
    vbuf,
    mbuf,
    bbuf,
    ibuf,
    kc,
    mc,
    lbuf,
    kb,
    gb,
    vt,
    acc,
    part,
    halo,
    rsh,
    fbuf,
    vsend,
    vrecv,
    bsend,
    brecv,
    isend,
    irecv,
    fsend,
    frecv,
    hsend,
    hrecv,
    local,
):
    phases, rows, cols = vol.shape[1:]
    groups = vbuf.shape[1] // 8
    nk = bank.shape[1]
    taken = SIDE * SIDE
    pad = SIDE // 2
    ext = rows + 2 * pad
    half = ext // 2
    full = phases // per
    reach = taps.shape[0] // 2
    me = lax.axis_index("depth")
    row = lax.axis_index("row")
    first = me * per
    has_prev = row > 0
    has_next = row < nrows - 1
    bounds = [i * groups // chunks for i in range(chunks + 1)]

    def peer(k):
        if count & (count - 1):
            return lax.rem(me + k, count)
        at, bit = 0, 1
        while bit < count:
            at = at + bit * lax.rem(lax.div(me, bit) + lax.div(k, bit), 2)
            bit *= 2
        return at

    def source(k):
        if count & (count - 1):
            return lax.rem(me + count - k, count)
        return peer(k)

    def others(body):
        def step(i, carry):
            body(count - 1 - i)
            return carry

        lax.fori_loop(0, count - 1, step, 0)

    def sized(d, c, body):
        low = bounds[c] * 8
        size = min(bounds[c + 1] * 8, per) - low
        tail = min(phases - full * per - low, size)

        @pl.when(d < full)
        def _():
            body(low, size)

        if tail > 0:

            @pl.when(d == full)
            def _():
                body(low, tail)

    def remote(src, dst, ssem, rsem, k):
        return pltpu.make_async_remote_copy(
            src_ref=src,
            dst_ref=dst,
            send_sem=ssem,
            recv_sem=rsem,
            device_id={"depth": peer(k)},
            device_id_type=MESH,
        )

    def vol_copy(k, slot, share, c, low, size):
        return remote(
            vol.at[0, pl.ds(share * per + low, size)],
            vbuf.at[slot, pl.ds(low, size)],
            vsend.at[c * count + k],
            vrecv.at[c * count + k],
            k,
        )

    def bank_copy(k, slot):
        return remote(bank.at[0], bbuf.at[slot], bsend.at[k], brecv.at[k], k)

    def idx_copy(k, slot):
        return remote(idx, ibuf.at[slot], isend.at[k], irecv.at[k], k)

    def out_copy(k, plane, share, c, low, size):
        return remote(
            fbuf.at[plane, pl.ds(low, size)],
            out.at[0, pl.ds(share * per + low, size)],
            fsend.at[c * count + k],
            frecv.at[c * count + k],
            k,
        )

    def own_vol(c, low, size):
        return pltpu.make_async_copy(
            vol.at[0, pl.ds(first + low, size)],
            vbuf.at[me, pl.ds(low, size)],
            local.at[4 * c],
        )

    def own_meas(c, low, size):
        return pltpu.make_async_copy(
            meas.at[pl.ds(first + low, size)], mbuf.at[pl.ds(low, size)], local.at[4 * c + 1]
        )

    def own_out(c, low, size):
        return pltpu.make_async_copy(
            fbuf.at[me, pl.ds(low, size)],
            out.at[0, pl.ds(first + low, size)],
            local.at[4 * c + 2],
        )

    own_bank = pltpu.make_async_copy(bank.at[0], bbuf.at[me], local.at[3])
    own_idx = pltpu.make_async_copy(idx, ibuf.at[me], local.at[4 * chunks])

    barrier = pltpu.get_barrier_semaphore()

    def greet(k):
        pl.semaphore_signal(
            barrier, inc=1, device_id={"depth": peer(k)}, device_id_type=MESH
        )

    others(greet)
    for other in (lax.rem(row + 1, nrows), lax.rem(row + nrows - 1, nrows)):
        pl.semaphore_signal(
            barrier, inc=1, device_id={"row": other}, device_id_type=MESH
        )

    own_bank.start()
    own_idx.start()
    for c in range(chunks):
        sized(me, c, lambda low, size: own_vol(c, low, size).start())
        sized(me, c, lambda low, size: own_meas(c, low, size).start())

    lane = lax.broadcasted_iota(jnp.int32, (8, phases), 1)
    sub = lax.broadcasted_iota(jnp.int32, (8, phases), 0)

    def picks(g):
        return lane == first + g * 8 + sub

    for g in range(groups):
        line = jnp.broadcast_to(lim[...], (8, phases))
        lbuf[g * 8 : g * 8 + 8, :] = jnp.broadcast_to(
            jnp.sum(jnp.where(picks(g), line, 0.0), axis=1, keepdims=True), (8, cols)
        )
    acc[...] = jnp.zeros_like(acc)

    pl.semaphore_wait(barrier, count + 1)

    def send_small(k):
        bank_copy(k, me).start()
        idx_copy(k, me).start()

    others(send_small)
    for c in range(chunks):

        def send_vol(k):
            share = peer(k)
            sized(
                share, c, lambda low, size: vol_copy(k, me, share, c, low, size).start()
            )

        others(send_vol)

    own_bank.wait()
    own_idx.wait()

    def small_in(k):
        bank_copy(k, source(k)).wait_recv()
        idx_copy(k, source(k)).wait_recv()

    others(small_in)

    def compact(z, carry):
        for g in range(groups):
            row_of = jnp.broadcast_to(ibuf[z], (8, phases))
            which = jnp.sum(
                jnp.where(picks(g), row_of.astype(jnp.float32), 0.0), axis=1, keepdims=True
            )
            total = jnp.zeros((8, taken), jnp.float32)
            for n in range(nk):
                line = jnp.broadcast_to(bbuf[z, n : n + 1, :], (8, taken))
                total = jnp.where(which == float(n), line, total)
            kc[z, g * 8 : g * 8 + 8, :] = total
        return carry

    lax.fori_loop(0, count, compact, 0)

    def spread(c):
        def plane(z, carry):
            for g in range(bounds[c], bounds[c + 1]):
                block = kc[z, g * 8 : g * 8 + 8, :]
                for ab in range(taken):
                    kb[z, ab, g * 8 : g * 8 + 8, :] = jnp.broadcast_to(
                        block[:, ab : ab + 1], (8, cols)
                    )
            return carry

        lax.fori_loop(0, count, plane, 0)

    def spread_mixed(c):
        for g in range(bounds[c], bounds[c + 1]):
            for zo in range(count):
                block = jnp.zeros((8, taken), jnp.float32)
                for z in range(max(0, zo - reach), min(count, zo + reach + 1)):
                    tap = STEP * taps[z - zo + reach]
                    block = block + tap * kc[z, g * 8 : g * 8 + 8, :]
                mc[zo, g * 8 : g * 8 + 8, :] = block

        def plane(z, carry):
            for g in range(bounds[c], bounds[c + 1]):
                block = mc[z, g * 8 : g * 8 + 8, :]
                for ab in range(taken):
                    gb[z, ab, g * 8 : g * 8 + 8, :] = jnp.broadcast_to(
                        block[:, ab : ab + 1], (8, cols)
                    )
            return carry

        lax.fori_loop(0, count, plane, 0)

    def at_group(g):
        return pl.ds(pl.multiple_of(g * 8, 8), 8)

    def project(z, c):
        def group(g, carry):
            at = at_group(g)
            lines = [vbuf[z, at, s, :] for s in range(rows)]
            for s in range(rows):
                vt[z, s, at, :] = lines[s]
            for b in range(SIDE):
                weight = [kb[z, a * SIDE + b, at, :] for a in range(SIDE)]
                for o in range(ext):
                    total = acc[b, o, at, :]
                    for a in range(SIDE):
                        s = o - 2 * pad + a
                        if 0 <= s < rows:
                            total = total + weight[a] * lines[s]
                    acc[b, o, at, :] = total
            return carry

        lax.fori_loop(bounds[c], bounds[c + 1], group, 0)

    t = lax.broadcasted_iota(jnp.int32, (8, cols), 1)

    def shifted(x, by):
        if by == 0:
            return x
        inside = (t + by >= 0) & (t + by < cols)
        return jnp.where(inside, pltpu.roll(x, (-by) % cols, 1), 0.0)

    def finish(c):
        def group(g, carry):
            at = at_group(g)
            for o in range(ext):
                total = acc[pad, o, at, :]
                for b in range(SIDE):
                    if b != pad:
                        total = total + shifted(acc[b, o, at, :], b - pad)
                if pad <= o < pad + rows:
                    part[o, at, :] = mbuf[at, o - pad, :] - total
                else:
                    part[o, at, :] = -total
            return carry

        lax.fori_loop(bounds[c], bounds[c + 1], group, 0)

    def rim(c, low, to, other):
        at = pl.ds(bounds[c] * 8, (bounds[c + 1] - bounds[c]) * 8)
        return pltpu.make_async_remote_copy(
            src_ref=part.at[pl.ds(low, half), at],
            dst_ref=halo.at[pl.ds(to, half), at],
            send_sem=hsend.at[2 * c + low // half],
            recv_sem=hrecv.at[2 * c + low // half],
            device_id={"row": lax.rem(row + other, nrows)},
            device_id_type=MESH,
        )

    def down(c):
        return rim(c, half, 0, 1)

    def up(c):
        return rim(c, 0, half, nrows - 1)

    def axial(c):
        def step(i, carry):
            at = at_group(lax.div(i, rows))
            s = lax.rem(i, rows)
            planes = [vt[z, s, at, :] for z in range(count)]
            for zo in range(count):
                total = None
                for z in range(max(0, zo - reach), min(count, zo + reach + 1)):
                    term = taps[z - zo + reach] * planes[z]
                    total = term if total is None else total + term
                vt[zo, s, at, :] = total
            return carry

        lax.fori_loop(bounds[c] * rows, bounds[c + 1] * rows, step, 0)

    def residual(c):
        def group(g, carry):
            at = at_group(g)
            for o in range(ext):
                there = has_prev if o < half else has_next
                got = jnp.where(there, halo[o, at, :], 0.0)
                total = part[o, at, :] + got
                if o < pad or o >= pad + rows:
                    total = jnp.where(there, total, 0.0)
                for b in range(SIDE):
                    rsh[b, o, at, :] = shifted(total, pad - b)
            return carry

        lax.fori_loop(bounds[c], bounds[c + 1], group, 0)

    def back(z, c):
        for g in range(bounds[c], bounds[c + 1]):
            at = pl.ds(g * 8, 8)
            totals = [vt[z, s, at, :] for s in range(rows)]
            for b in range(SIDE):
                shift = [rsh[b, o, at, :] for o in range(ext)]
                for a in range(SIDE):
                    weight = gb[z, a * SIDE + b, at, :]
                    for s in range(rows):
                        totals[s] = totals[s] + weight * shift[s - a + 2 * pad]
            limit = lbuf[at, :]
            for s in range(rows):
                value = totals[s]
                size = jnp.maximum(jnp.abs(value) - limit, 0.0)
                fbuf[z, at, s, :] = jnp.where(value < 0.0, -size, size)

    def forward(c):
        sized(me, c, lambda low, size: own_vol(c, low, size).wait())
        project(me, c)

        def arrive(k):
            sized(
                me, c, lambda low, size: vol_copy(k, source(k), me, c, low, size).wait_recv()
            )
            project(source(k), c)

        others(arrive)
        sized(me, c, lambda low, size: own_meas(c, low, size).wait())
        finish(c)

        @pl.when(has_next)
        def _():
            down(c).start()

        @pl.when(has_prev)
        def _():
            up(c).start()

    def backward(c):
        @pl.when(has_prev)
        def _():
            down(c).wait_recv()

        @pl.when(has_next)
        def _():
            up(c).wait_recv()

        residual(c)

        def give(k):
            back(peer(k), c)
            sized(
                me, c, lambda low, size: out_copy(k, peer(k), me, c, low, size).start()
            )

        others(give)
        back(me, c)
        sized(me, c, lambda low, size: own_out(c, low, size).start())

    spread(0)
    for c in range(chunks):
        forward(c)
        axial(c)
        spread_mixed(c)
        if c + 1 < chunks:
            spread(c + 1)
        backward(c)

    def drain(k):
        bank_copy(k, me).wait_send()
        idx_copy(k, me).wait_send()

    others(drain)
    for c in range(chunks):

        def drained(k):
            share = peer(k)
            sized(
                share, c, lambda low, size: vol_copy(k, me, share, c, low, size).wait_send()
            )
            sized(
                me, c, lambda low, size: out_copy(k, share, me, c, low, size).wait_send()
            )

        others(drained)

        @pl.when(has_next)
        def _():
            down(c).wait_send()

        @pl.when(has_prev)
        def _():
            up(c).wait_send()

        sized(me, c, lambda low, size: own_out(c, low, size).wait())
    for c in range(chunks):

        def collect(k):
            share = source(k)
            sized(
                share, c, lambda low, size: out_copy(k, me, share, c, low, size).wait_recv()
            )

        others(collect)


def shards(count, nrows, volume, measured, kernel_bank, kernel_index, taps, thresholds):
    planes, phases, rows, cols = volume.shape
    nk, size = kernel_bank.shape[1:]
    per = -(-phases // count)
    wide = -(-per // 8) * 8
    ext = rows + SIDE - 1
    f32 = jnp.float32
    dma = pltpu.SemaphoreType.DMA
    vmem = pl.BlockSpec(memory_space=pltpu.VMEM)
    smem = pl.BlockSpec(memory_space=pltpu.SMEM)
    hbm = pl.BlockSpec(memory_space=pl.ANY)
    chunks = min(CHUNKS, wide // 8)
    return pl.pallas_call(
        functools.partial(kernel, count, nrows, per, chunks),
        out_shape=jax.ShapeDtypeStruct(volume.shape, f32),
        in_specs=[hbm, hbm, vmem, vmem, smem, vmem],
        out_specs=hbm,
        scratch_shapes=[
            pltpu.VMEM((count, wide, rows, cols), f32),
            pltpu.VMEM((wide, rows, cols), f32),
            pltpu.VMEM((count, nk, size), f32),
            pltpu.VMEM((count, 1, phases), jnp.int32),
            pltpu.VMEM((count, wide, size), f32),
            pltpu.VMEM((count, wide, size), f32),
            pltpu.VMEM((wide, cols), f32),
            pltpu.VMEM((count, size, wide, cols), f32),
            pltpu.VMEM((count, size, wide, cols), f32),
            pltpu.VMEM((count, rows, wide, cols), f32),
            pltpu.VMEM((SIDE, ext, wide, cols), f32),
            pltpu.VMEM((ext, wide, cols), f32),
            pltpu.VMEM((ext, wide, cols), f32),
            pltpu.VMEM((SIDE, ext, wide, cols), f32),
            pltpu.VMEM((count, wide, rows, cols), f32),
        ]
        + [dma((chunks * count,)), dma((chunks * count,))]
        + [dma((count,)) for _ in range(4)]
        + [dma((chunks * count,)), dma((chunks * count,))]
        + [dma((2 * chunks,)), dma((2 * chunks,)), dma((4 * chunks + 1,))],
        compiler_params=pltpu.CompilerParams(collective_id=0, has_side_effects=True),
    )(volume, measured, kernel_bank, kernel_index, taps, thresholds[None, :])


def solution(mesh):
    placed = (
        P("depth", None, "row", None),
        P(None, "row", None),
        P("depth", None, None),
        P("depth", None),
        P(),
        P(),
    )
    body = functools.partial(shards, mesh.shape["depth"], mesh.shape["row"])
    return jax.shard_map(
        body, mesh=mesh, in_specs=placed, out_specs=P("depth", None, "row", None), check_vma=False
    )
```

```python
import functools

import jax
import jax.numpy as jnp
from jax import lax
from jax.experimental import pallas as pl
from jax.experimental.pallas import tpu as pltpu
from jax.sharding import PartitionSpec as P

STEP = 4.0
SIDE = 5
CHUNKS = 2
MESH = pl.DeviceIdType.MESH


def kernel(
    count,
    nrows,
    per,
    chunks,
    vol,
    meas,
    bank,
    idx,
    taps,
    lim,
    out,
    vbuf,
    mbuf,
    msg,
    mbox,
    kc,
    mc,
    lbuf,
    kb,
    gb,
    vt,
    acc,
    part,
    halo,
    rsh,
    fbuf,
    vsend,
    vrecv,
    msend,
    mrecv,
    fsend,
    frecv,
    hsend,
    hrecv,
    local,
):
    phases, rows, cols = vol.shape[1:]
    groups = vbuf.shape[1] // 8
    nk = bank.shape[1]
    taken = SIDE * SIDE
    pad = SIDE // 2
    ext = rows + 2 * pad
    half = ext // 2
    full = phases // per
    reach = taps.shape[0] // 2
    wide_lane = msg.shape[1]
    room = 32
    fit = wide_lane // room
    bank_rows = -(-nk // fit)
    idx_rows = msg.shape[0] - bank_rows
    me = lax.axis_index("depth")
    row = lax.axis_index("row")
    first = me * per
    has_prev = row > 0
    has_next = row < nrows - 1
    bounds = [i * groups // chunks for i in range(chunks + 1)]

    def peer(k):
        if count & (count - 1):
            return lax.rem(me + k, count)
        at, bit = 0, 1
        while bit < count:
            at = at + bit * lax.rem(lax.div(me, bit) + lax.div(k, bit), 2)
            bit *= 2
        return at

    def source(k):
        if count & (count - 1):
            return lax.rem(me + count - k, count)
        return peer(k)

    def others(body):
        def step(i, carry):
            body(count - 1 - i)
            return carry

        lax.fori_loop(0, count - 1, step, 0)

    def sized(d, c, body):
        low = bounds[c] * 8
        size = min(bounds[c + 1] * 8, per) - low
        tail = min(phases - full * per - low, size)

        @pl.when(d < full)
        def _():
            body(low, size)

        if tail > 0:

            @pl.when(d == full)
            def _():
                body(low, tail)

    def remote(src, dst, ssem, rsem, k):
        return pltpu.make_async_remote_copy(
            src_ref=src,
            dst_ref=dst,
            send_sem=ssem,
            recv_sem=rsem,
            device_id={"depth": peer(k)},
            device_id_type=MESH,
        )

    def vol_copy(k, slot, share, c, low, size):
        return remote(
            vol.at[0, pl.ds(share * per + low, size)],
            vbuf.at[slot, pl.ds(low, size)],
            vsend.at[c * count + k],
            vrecv.at[c * count + k],
            k,
        )

    def msg_copy(k, slot):
        return remote(msg, mbox.at[slot], msend.at[k], mrecv.at[k], k)

    def out_copy(k, plane, share, c, low, size):
        return remote(
            fbuf.at[plane, pl.ds(low, size)],
            out.at[0, pl.ds(share * per + low, size)],
            fsend.at[c * count + k],
            frecv.at[c * count + k],
            k,
        )

    def own_vol(c, low, size):
        return pltpu.make_async_copy(
            vol.at[0, pl.ds(first + low, size)],
            vbuf.at[me, pl.ds(low, size)],
            local.at[4 * c],
        )

    def own_meas(c, low, size):
        return pltpu.make_async_copy(
            meas.at[pl.ds(first + low, size)], mbuf.at[pl.ds(low, size)], local.at[4 * c + 1]
        )

    def own_out(c, low, size):
        return pltpu.make_async_copy(
            fbuf.at[me, pl.ds(low, size)],
            out.at[0, pl.ds(first + low, size)],
            local.at[4 * c + 2],
        )

    own_msg = pltpu.make_async_copy(msg, mbox.at[me], local.at[3])

    barrier = pltpu.get_barrier_semaphore()

    def greet(k):
        pl.semaphore_signal(
            barrier, inc=1, device_id={"depth": peer(k)}, device_id_type=MESH
        )

    others(greet)
    for other in (lax.rem(row + 1, nrows), lax.rem(row + nrows - 1, nrows)):
        pl.semaphore_signal(
            barrier, inc=1, device_id={"row": other}, device_id_type=MESH
        )

    msg[...] = jnp.zeros_like(msg)
    for n in range(nk):
        r, c = n // fit, n % fit * room
        msg[r : r + 1, c : c + taken] = bank[0, n : n + 1, :]
    numbers = idx[...].astype(jnp.float32)
    for r in range(idx_rows):
        c = min(phases - r * wide_lane, wide_lane)
        msg[bank_rows + r : bank_rows + r + 1, 0:c] = numbers[
            :, r * wide_lane : r * wide_lane + c
        ]

    for c in range(chunks):
        sized(me, c, lambda low, size: own_vol(c, low, size).start())
        sized(me, c, lambda low, size: own_meas(c, low, size).start())

    lane = lax.broadcasted_iota(jnp.int32, (8, phases), 1)
    sub = lax.broadcasted_iota(jnp.int32, (8, phases), 0)

    def picks(g):
        return lane == first + g * 8 + sub

    for g in range(groups):
        line = jnp.broadcast_to(lim[...], (8, phases))
        lbuf[g * 8 : g * 8 + 8, :] = jnp.broadcast_to(
            jnp.sum(jnp.where(picks(g), line, 0.0), axis=1, keepdims=True), (8, cols)
        )
    acc[...] = jnp.zeros_like(acc)

    pl.semaphore_wait(barrier, count + 1)

    own_msg.start()
    others(lambda k: msg_copy(k, me).start())
    for c in range(chunks):

        def send_vol(k):
            share = peer(k)
            sized(
                share, c, lambda low, size: vol_copy(k, me, share, c, low, size).start()
            )

        others(send_vol)

    own_msg.wait()
    others(lambda k: msg_copy(k, source(k)).wait_recv())

    lane_of = lax.broadcasted_iota(jnp.int32, (8, wide_lane), 1)
    sub_of = lax.broadcasted_iota(jnp.int32, (8, wide_lane), 0)

    def compact(c):
        def plane(z, carry):
            lines = []
            for n in range(nk):
                r, at = n // fit, n % fit * room
                line = mbox[z, r : r + 1, at : at + taken]
                lines.append(jnp.broadcast_to(line, (8, taken)))
            for g in range(bounds[c], bounds[c + 1]):
                found = jnp.zeros((8, wide_lane), jnp.float32)
                for r in range(idx_rows):
                    numbers = jnp.broadcast_to(
                        mbox[z, bank_rows + r : bank_rows + r + 1, :], (8, wide_lane)
                    )
                    here = lane_of + r * wide_lane == first + g * 8 + sub_of
                    found = jnp.where(here, numbers, found)
                which = jnp.sum(found, axis=1, keepdims=True)
                total = jnp.zeros((8, taken), jnp.float32)
                for n in range(nk):
                    total = jnp.where(which == float(n), lines[n], total)
                kc[z, g * 8 : g * 8 + 8, :] = total
            return carry

        lax.fori_loop(0, count, plane, 0, unroll=4 if count % 4 == 0 else 1)

    def spread(c):
        def plane(z, carry):
            for g in range(bounds[c], bounds[c + 1]):
                block = kc[z, g * 8 : g * 8 + 8, :]
                for ab in range(taken):
                    kb[z, ab, g * 8 : g * 8 + 8, :] = jnp.broadcast_to(
                        block[:, ab : ab + 1], (8, cols)
                    )
            return carry

        lax.fori_loop(0, count, plane, 0)

    def spread_mixed(c):
        for g in range(bounds[c], bounds[c + 1]):
            for zo in range(count):
                block = jnp.zeros((8, taken), jnp.float32)
                for z in range(max(0, zo - reach), min(count, zo + reach + 1)):
                    tap = STEP * taps[z - zo + reach]
                    block = block + tap * kc[z, g * 8 : g * 8 + 8, :]
                mc[zo, g * 8 : g * 8 + 8, :] = block

        def plane(z, carry):
            for g in range(bounds[c], bounds[c + 1]):
                block = mc[z, g * 8 : g * 8 + 8, :]
                for ab in range(taken):
                    gb[z, ab, g * 8 : g * 8 + 8, :] = jnp.broadcast_to(
                        block[:, ab : ab + 1], (8, cols)
                    )
            return carry

        lax.fori_loop(0, count, plane, 0)

    def at_group(g):
        return pl.ds(pl.multiple_of(g * 8, 8), 8)

    def project(z, c):
        def group(g, carry):
            at = at_group(g)
            lines = [vbuf[z, at, s, :] for s in range(rows)]
            for s in range(rows):
                vt[z, s, at, :] = lines[s]
            for b in range(SIDE):
                weight = [kb[z, a * SIDE + b, at, :] for a in range(SIDE)]
                for o in range(ext):
                    total = acc[b, o, at, :]
                    for a in range(SIDE):
                        s = o - 2 * pad + a
                        if 0 <= s < rows:
                            total = total + weight[a] * lines[s]
                    acc[b, o, at, :] = total
            return carry

        lax.fori_loop(bounds[c], bounds[c + 1], group, 0)

    t = lax.broadcasted_iota(jnp.int32, (8, cols), 1)

    def shifted(x, by):
        if by == 0:
            return x
        inside = (t + by >= 0) & (t + by < cols)
        return jnp.where(inside, pltpu.roll(x, (-by) % cols, 1), 0.0)

    def finish(c):
        def group(g, carry):
            at = at_group(g)
            for o in range(ext):
                total = acc[pad, o, at, :]
                for b in range(SIDE):
                    if b != pad:
                        total = total + shifted(acc[b, o, at, :], b - pad)
                if pad <= o < pad + rows:
                    part[o, at, :] = mbuf[at, o - pad, :] - total
                else:
                    part[o, at, :] = -total
            return carry

        lax.fori_loop(bounds[c], bounds[c + 1], group, 0)

    def rim(c, low, to, other):
        at = pl.ds(bounds[c] * 8, (bounds[c + 1] - bounds[c]) * 8)
        return pltpu.make_async_remote_copy(
            src_ref=part.at[pl.ds(low, half), at],
            dst_ref=halo.at[pl.ds(to, half), at],
            send_sem=hsend.at[2 * c + low // half],
            recv_sem=hrecv.at[2 * c + low // half],
            device_id={"row": lax.rem(row + other, nrows)},
            device_id_type=MESH,
        )

    def down(c):
        return rim(c, half, 0, 1)

    def up(c):
        return rim(c, 0, half, nrows - 1)

    def axial(c):
        def step(i, carry):
            at = at_group(lax.div(i, rows))
            s = lax.rem(i, rows)
            planes = [vt[z, s, at, :] for z in range(count)]
            for zo in range(count):
                total = None
                for z in range(max(0, zo - reach), min(count, zo + reach + 1)):
                    term = taps[z - zo + reach] * planes[z]
                    total = term if total is None else total + term
                vt[zo, s, at, :] = total
            return carry

        lax.fori_loop(bounds[c] * rows, bounds[c + 1] * rows, step, 0)

    def residual(c):
        def group(g, carry):
            at = at_group(g)
            for o in range(ext):
                there = has_prev if o < half else has_next
                got = jnp.where(there, halo[o, at, :], 0.0)
                total = part[o, at, :] + got
                if o < pad or o >= pad + rows:
                    total = jnp.where(there, total, 0.0)
                for b in range(SIDE):
                    rsh[b, o, at, :] = shifted(total, pad - b)
            return carry

        lax.fori_loop(bounds[c], bounds[c + 1], group, 0)

    def back(z, c):
        for g in range(bounds[c], bounds[c + 1]):
            at = pl.ds(g * 8, 8)
            totals = [vt[z, s, at, :] for s in range(rows)]
            for b in range(SIDE):
                shift = [rsh[b, o, at, :] for o in range(ext)]
                for a in range(SIDE):
                    weight = gb[z, a * SIDE + b, at, :]
                    for s in range(rows):
                        totals[s] = totals[s] + weight * shift[s - a + 2 * pad]
            limit = lbuf[at, :]
            for s in range(rows):
                value = totals[s]
                size = jnp.maximum(jnp.abs(value) - limit, 0.0)
                fbuf[z, at, s, :] = jnp.where(value < 0.0, -size, size)

    def forward(c):
        sized(me, c, lambda low, size: own_vol(c, low, size).wait())
        project(me, c)

        def arrive(k):
            sized(
                me, c, lambda low, size: vol_copy(k, source(k), me, c, low, size).wait_recv()
            )
            project(source(k), c)

        others(arrive)
        sized(me, c, lambda low, size: own_meas(c, low, size).wait())
        finish(c)

        @pl.when(has_next)
        def _():
            down(c).start()

        @pl.when(has_prev)
        def _():
            up(c).start()

    def backward(c):
        @pl.when(has_prev)
        def _():
            down(c).wait_recv()

        @pl.when(has_next)
        def _():
            up(c).wait_recv()

        residual(c)

        def give(k):
            back(peer(k), c)
            sized(
                me, c, lambda low, size: out_copy(k, peer(k), me, c, low, size).start()
            )

        others(give)
        back(me, c)
        sized(me, c, lambda low, size: own_out(c, low, size).start())

    compact(0)
    spread(0)
    for c in range(chunks):
        forward(c)
        axial(c)
        if c == 0:
            spread_mixed(0)
        if c + 1 < chunks:
            compact(c + 1)
            spread(c + 1)
        backward(c)
        if c + 1 < chunks:
            spread_mixed(c + 1)

    others(lambda k: msg_copy(k, me).wait_send())
    for c in range(chunks):

        def drained(k):
            share = peer(k)
            sized(
                share, c, lambda low, size: vol_copy(k, me, share, c, low, size).wait_send()
            )
            sized(
                me, c, lambda low, size: out_copy(k, share, me, c, low, size).wait_send()
            )

        others(drained)

        @pl.when(has_next)
        def _():
            down(c).wait_send()

        @pl.when(has_prev)
        def _():
            up(c).wait_send()

        sized(me, c, lambda low, size: own_out(c, low, size).wait())
    for c in range(chunks):

        def collect(k):
            share = source(k)
            sized(
                share, c, lambda low, size: out_copy(k, me, share, c, low, size).wait_recv()
            )

        others(collect)


def shards(count, nrows, volume, measured, kernel_bank, kernel_index, taps, thresholds):
    planes, phases, rows, cols = volume.shape
    nk, size = kernel_bank.shape[1:]
    per = -(-phases // count)
    wide = -(-per // 8) * 8
    ext = rows + SIDE - 1
    f32 = jnp.float32
    dma = pltpu.SemaphoreType.DMA
    vmem = pl.BlockSpec(memory_space=pltpu.VMEM)
    smem = pl.BlockSpec(memory_space=pltpu.SMEM)
    hbm = pl.BlockSpec(memory_space=pl.ANY)
    chunks = min(CHUNKS, wide // 8)
    lines = -(-nk // (cols // 32)) + -(-phases // cols)
    return pl.pallas_call(
        functools.partial(kernel, count, nrows, per, chunks),
        out_shape=pltpu.VMEM(volume.shape, f32),
        in_specs=[hbm, hbm, vmem, vmem, smem, vmem],
        out_specs=vmem,
        scratch_shapes=[
            pltpu.VMEM((count, wide, rows, cols), f32),
            pltpu.VMEM((wide, rows, cols), f32),
            pltpu.VMEM((lines, cols), f32),
            pltpu.VMEM((count, lines, cols), f32),
            pltpu.VMEM((count, wide, size), f32),
            pltpu.VMEM((count, wide, size), f32),
            pltpu.VMEM((wide, cols), f32),
            pltpu.VMEM((count, size, wide, cols), f32),
            pltpu.VMEM((count, size, wide, cols), f32),
            pltpu.VMEM((count, rows, wide, cols), f32),
            pltpu.VMEM((SIDE, ext, wide, cols), f32),
            pltpu.VMEM((ext, wide, cols), f32),
            pltpu.VMEM((ext, wide, cols), f32),
            pltpu.VMEM((SIDE, ext, wide, cols), f32),
            pltpu.VMEM((count, wide, rows, cols), f32),
        ]
        + [dma((chunks * count,)), dma((chunks * count,))]
        + [dma((count,)) for _ in range(2)]
        + [dma((chunks * count,)), dma((chunks * count,))]
        + [dma((2 * chunks,)), dma((2 * chunks,)), dma((4 * chunks,))],
        compiler_params=pltpu.CompilerParams(collective_id=0, has_side_effects=True),
    )(volume, measured, kernel_bank, kernel_index, taps, thresholds[None, :])


def solution(mesh):
    placed = (
        P("depth", None, "row", None),
        P(None, "row", None),
        P("depth", None, None),
        P("depth", None),
        P(),
        P(),
    )
    body = functools.partial(shards, mesh.shape["depth"], mesh.shape["row"])
    return jax.shard_map(
        body, mesh=mesh, in_specs=placed, out_specs=P("depth", None, "row", None), check_vma=False
    )
```
